128 devices in a mesh: grp: 16 (over z, y), mem: 8 (over x, core).
Axes of the slice: x: 4, y: 4, z: 4, core: 2. Of those that a mesh axis runs over, the one named last changes fastest.
Arguments:
- blocks: bfloat16 [1536, 27, 128, 128], P(('grp', 'mem'))
- prolong: bfloat16 [1536, 128, 128], P(('grp', 'mem'))
- cols: int32 [1536, 27], P(('grp', 'mem')), may hold values from 0 to 11, as said below
- codes: int32 [1536], P(('grp', 'mem')), may hold values from 1 to 15, as said below
Outputs:
- coarse_rows: bfloat16 [1536, 27, 128, 128], P(('grp', 'mem'))
- diag_inverse: float32 [1536, 128, 128], P('grp', 'mem')
The draws below stay inside these ranges and needn't reach their ends.
Inputs may be any that keep to these rules, and one draw needn't show every extreme that they name: codes is the same for the fine rows in slot s of partition m of every group, and the codes of one device's 12 rows are distinct, so the matching is symmetric and a device pairs with each other group at most once. Entry 13 of every row of cols is the row's own slot.
All inputs are finite; a program needn't handle non-finite values.
Results may differ from the reference program's by a relative error of at most 0.0036.
Values may be sent and summed in bfloat16 or wider, within the bound.
No kernel may reach another device: no remote copies, remote signals or barrier semaphores. Data moves between devices by JAX's collectives and lax.ppermute only.
A program may use at most 128 MiB of HBM per device.

```python
import jax
import jax.numpy as jnp
from jax import lax

B = 128
K = 27
ROW_DEV = 12
NEWTON = 2
ROWS = 1536
N_GRP = 16
N_MEM = 8


def draw_blocks(key, part):
    noise = jax.random.normal(key, (ROWS, K, B, B), jnp.float32) * (0.5 / B ** 0.5)
    center = (jnp.arange(K) == 13).astype(jnp.float32)
    diag_vals = jax.random.uniform(jax.random.fold_in(key, 7), (ROWS, 1, B, 1), jnp.float32, 2.0, 4.0)
    eye = jnp.eye(B, dtype=jnp.float32)
    return (noise + center[None, :, None, None] * eye[None, None] * diag_vals).astype(jnp.bfloat16)


def draw_prolong(key, part):
    noise = jax.random.normal(key, (ROWS, B, B), jnp.float32) * (0.3 / B ** 0.5)
    return (jnp.eye(B, dtype=jnp.float32)[None] + noise).astype(jnp.bfloat16)


def draw_cols(key, part):
    picks = jax.random.randint(key, (ROWS, K), 0, ROW_DEV).astype(jnp.int32)
    own_slot = (jnp.arange(ROWS, dtype=jnp.int32) % ROW_DEV)[:, None]
    center = (jnp.arange(K, dtype=jnp.int32) == 13)[None, :]
    return jnp.where(center, own_slot, picks).astype(jnp.int32)


def draw_codes(key, part):

    def one_member(member):
        order = jax.random.permutation(jax.random.fold_in(key, member), N_GRP - 1)
        return order[:ROW_DEV].astype(jnp.int32) + 1
    table = jax.vmap(one_member)(jnp.arange(N_MEM, dtype=jnp.int32))
    return jnp.broadcast_to(table[None], (N_GRP, N_MEM, ROW_DEV)).reshape(ROWS).astype(jnp.int32)


def setup_inputs(seed: int = 0) -> dict:
    streams_of = jax.random.split(jax.random.key(seed), 5)
    return {
        "blocks": draw_blocks(jax.random.fold_in(streams_of[4], 71), 0),
        "prolong": draw_prolong(jax.random.fold_in(streams_of[4], 71), 0),
        "cols": draw_cols(jax.random.fold_in(streams_of[4], 71), 0),
        "codes": draw_codes(jax.random.fold_in(streams_of[4], 71), 0),
    }


def newton_inverse(dmat):
    eye = jnp.eye(dmat.shape[0], dtype=jnp.float32)
    approx = eye * (1.0 / jnp.diagonal(dmat))[:, None]
    for step in range(NEWTON):
        inner = jnp.dot(dmat, approx, precision=lax.Precision.HIGHEST)
        approx = jnp.dot(approx, 2.0 * eye - inner, precision=lax.Precision.HIGHEST)
    return approx


def reference(blocks, prolong, cols, codes):
    rows = blocks.shape[0]
    index = jnp.arange(rows, dtype=jnp.int32)
    base = (index // ROW_DEV) * ROW_DEV
    global_cols = (base[:, None] + cols).astype(jnp.int32)
    span = N_MEM * ROW_DEV
    partner = ((index // span) ^ codes) * span + index % span

    def right_row(r):
        left_blocks = blocks[r].astype(jnp.float32)
        right_blocks = prolong[global_cols[r]].astype(jnp.float32)
        return jnp.einsum("kab,kbc->kac", left_blocks, right_blocks).astype(jnp.bfloat16)

    right = lax.map(right_row, index)

    def term_row(r):
        return jnp.einsum("ba,kbc->kac", prolong[r].astype(jnp.float32), right[r].astype(jnp.float32))

    def coarse_row(r):
        total = term_row(r) + term_row(partner[r])
        return total.astype(jnp.bfloat16), newton_inverse(total[13])

    coarse_rows, diag_inverse = lax.map(coarse_row, index)
    return coarse_rows, diag_inverse
```

```python
import functools

import jax
import jax.numpy as jnp
from jax import lax
from jax.experimental import pallas as pl
from jax.experimental.pallas import tpu as pltpu
from jax.sharding import PartitionSpec as P


F32, BF16 = jnp.float32, jnp.bfloat16
DIAG = 13
LINKS = (1, 3, 4, 12)
ROUNDS = (
    (13, 3, 10, 12),
    (1, 15, 9, 14),
    (10, 6, 4, 13),
    (9, 14, 11, 15),
    (2, 10, 7, 8),
    (5, 11, 6, 9),
    (14, 7, 8, 10),
    (6, 2, 5, 11),
)
CALLS = ((13, 3, 10, 12), (1, 15, 9, 14), (6, 4, 11, 2, 7, 8, 5))
LAST = {code: r for r, row in enumerate(ROUNDS) for code in row}


def pick(i, values):
    out = jnp.int32(values[0])
    for j, v in enumerate(values[1:], 1):
        out = jnp.where(i == j, jnp.int32(v), out)
    return out


def slot_of(codes_ref, code, rows):
    slot = jnp.int32(0)
    for s in range(rows):
        slot = jnp.where(codes_ref[s] == code, jnp.int32(s), slot)
    return slot


def has_code(codes_ref, code, rows):
    found = codes_ref[0] == code
    for s in range(1, rows):
        found = found | (codes_ref[s] == code)
    return found


def transposed(x):
    return x.astype(F32).T.astype(BF16)


def term_kernel(group, rows, ks, codes_ref, cols_ref, blocks_ref, prolong_ref, *refs):
    n = len(group)
    outs, own_ref, buf, sem = refs[:n], refs[n], refs[n + 1], refs[n + 2]
    i = pl.program_id(0)
    code = pick(i, group)
    slot = slot_of(codes_ref, code, rows)

    @pl.when(has_code(codes_ref, code, rows))
    def _():
        left = transposed(prolong_ref[slot])
        for a in range(0, len(ks), 2):
            right = [
                jnp.dot(
                    blocks_ref[0, k], prolong_ref[cols_ref[slot, k]], preferred_element_type=F32
                ).astype(BF16)
                for k in ks[a : a + 2]
            ]
            term = jnp.dot(left, jnp.concatenate(right, axis=1), preferred_element_type=F32)
            for b in range(2):
                part = term[:, b * 128 : (b + 1) * 128]
                own_ref[0, a + b] = part
                buf[i, a + b] = part.astype(BF16)

    for j in range(n):
        @pl.when(i == j)
        def _():
            pltpu.make_async_copy(buf.at[j], outs[j], sem.at[j]).start()

    @pl.when(i == n - 1)
    def _():
        for j in range(n):
            pltpu.make_async_copy(buf.at[j], outs[j], sem.at[j]).wait()


def terms(group, ks, codes, cols, blocks, prolong):
    rows, width, b, _ = blocks.shape
    n, m = len(group), len(ks)
    spec = pltpu.PrefetchScalarGridSpec(
        num_scalar_prefetch=2,
        grid=(n,),
        in_specs=[
            pl.BlockSpec(
                (1, width, b, b),
                lambda i, codes, cols: (slot_of(codes, pick(i, group), rows), 0, 0, 0),
            ),
            pl.BlockSpec((rows, b, b), lambda i, codes, cols: (0, 0, 0)),
        ],
        out_specs=[pl.BlockSpec(memory_space=pl.ANY)] * n
        + [pl.BlockSpec((1, m, b, b), lambda i, codes, cols: (i, 0, 0, 0))],
        scratch_shapes=[pltpu.VMEM((n, m, b, b), BF16), pltpu.SemaphoreType.DMA((n,))],
    )
    flops = n * m * 4 * b**3
    out = pl.pallas_call(
        functools.partial(term_kernel, group, rows, ks),
        grid_spec=spec,
        out_shape=[jax.ShapeDtypeStruct((m, b, b), BF16)] * n
        + [jax.ShapeDtypeStruct((n, m, b, b), F32)],
        cost_estimate=pl.CostEstimate(
            flops=flops, bytes_accessed=n * m * b * b * 8, transcendentals=0
        ),
        name=f"terms{len(group)}",
    )(codes, cols, blocks, prolong)
    return out[:n], out[n]


def diag_kernel(rows, codes_ref, place_ref, blocks_ref, prolong_ref, send_ref, own_ref):
    for s in range(rows):
        right = jnp.dot(blocks_ref[s, 0], prolong_ref[s], preferred_element_type=F32).astype(BF16)
        term = jnp.dot(transposed(prolong_ref[s]), right, preferred_element_type=F32)
        own_ref[s] = term
        send_ref[place_ref[0] ^ codes_ref[s]] = term.astype(BF16)


def diag_terms(groups, codes, place, blocks, prolong):
    rows, _, b, _ = blocks.shape
    spec = pltpu.PrefetchScalarGridSpec(
        num_scalar_prefetch=2,
        grid=(1,),
        in_specs=[
            pl.BlockSpec((rows, 1, b, b), lambda i, *_: (0, DIAG, 0, 0)),
            pl.BlockSpec((rows, b, b), lambda i, *_: (0, 0, 0)),
        ],
        out_specs=[
            pl.BlockSpec((groups, b, b), lambda i, *_: (0, 0, 0)),
            pl.BlockSpec((rows, b, b), lambda i, *_: (0, 0, 0)),
        ],
    )
    return pl.pallas_call(
        functools.partial(diag_kernel, rows),
        grid_spec=spec,
        out_shape=[
            jax.ShapeDtypeStruct((groups, b, b), BF16),
            jax.ShapeDtypeStruct((rows, b, b), F32),
        ],
        cost_estimate=pl.CostEstimate(
            flops=rows * 4 * b**3, bytes_accessed=rows * b * b * 10, transcendentals=0
        ),
        name="diag_terms",
    )(codes, place, blocks, prolong)


def inverse_kernel(rows, parts, codes_ref, place_ref, own_ref, arrived_ref, coarse_ref, inv_ref):
    b = own_ref.shape[1]
    share = b // parts
    row = lax.broadcasted_iota(jnp.int32, (b, b), 0)
    col = lax.broadcasted_iota(jnp.int32, (b, b), 1)
    on_diag = row == col
    two_eye = jnp.where(on_diag, 2.0, 0.0).astype(F32)
    dot = functools.partial(
        jnp.dot, precision=lax.Precision.HIGHEST, preferred_element_type=F32
    )
    for s in range(rows):
        d = own_ref[s] + arrived_ref[place_ref[0] ^ codes_ref[s]].astype(F32)
        coarse_ref[s, 0] = d.astype(BF16)
        only = jnp.where(on_diag, d, 0.0)
        by_col = 1.0 / jnp.sum(only, axis=0, keepdims=True)
        by_row = 1.0 / jnp.sum(only, axis=1, keepdims=True)
        x = by_row * (two_eye - d * by_col)
        x = dot(x, two_eye - dot(d, x))
        for j in range(parts):
            inv_ref[j, s] = x[j * share : (j + 1) * share]


def inverses(parts, codes, place, own, arrived, width):
    rows, b, _ = own.shape
    spec = pltpu.PrefetchScalarGridSpec(
        num_scalar_prefetch=2,
        grid=(1,),
        in_specs=[
            pl.BlockSpec(own.shape, lambda i, *_: (0, 0, 0)),
            pl.BlockSpec(arrived.shape, lambda i, *_: (0, 0, 0)),
        ],
        out_specs=[
            pl.BlockSpec((rows, 1, b, b), lambda i, *_: (0, DIAG, 0, 0)),
            pl.BlockSpec((parts, rows, b // parts, b), lambda i, *_: (0, 0, 0, 0)),
        ],
    )
    return pl.pallas_call(
        functools.partial(inverse_kernel, rows, parts),
        grid_spec=spec,
        out_shape=[
            jax.ShapeDtypeStruct((rows, width, b, b), BF16),
            jax.ShapeDtypeStruct((parts, rows, b // parts, b), F32),
        ],
        cost_estimate=pl.CostEstimate(
            flops=rows * 24 * b**3, bytes_accessed=rows * b * b * 12, transcendentals=0
        ),
        name="inverses",
    )(codes, place, own, arrived)


def add_kernel(group, places, rows, n_own, codes_ref, *refs):
    n = len(group)
    arrived = refs[:n]
    own = refs[n : n + n_own]
    coarse = refs[n + n_own + 1]
    buf_in, buf_own, buf_out, sem_in, sem_own, sem_out = refs[n + n_own + 2 :]
    m = buf_in.shape[1]
    half = m // 2

    def copies(j, h, slot):
        part = pl.ds(h * half, half)
        which, at = places[j]
        return (
            pltpu.make_async_copy(arrived[j].at[part], buf_in.at[j, part], sem_in.at[j, h]),
            pltpu.make_async_copy(
                own[which].at[at, part], buf_own.at[j, part], sem_own.at[j, h]
            ),
            pltpu.make_async_copy(
                buf_out.at[j, part],
                coarse.at[slot, pl.ds(h * (half + 1), half)],
                sem_out.at[j, h],
            ),
        )

    slots = [slot_of(codes_ref, code, rows) for code in group]
    found = [has_code(codes_ref, code, rows) for code in group]
    for j in range(n):
        @pl.when(found[j])
        def _():
            for h in range(2):
                take, mine, _ = copies(j, h, slots[j])
                take.start()
                mine.start()
    for j in range(n):
        @pl.when(found[j])
        def _():
            for h in range(2):
                take, mine, put = copies(j, h, slots[j])
                take.wait()
                mine.wait()
                for k in range(h * half, (h + 1) * half):
                    buf_out[j, k] = (buf_own[j, k] + buf_in[j, k].astype(F32)).astype(BF16)
                put.start()
    for j in range(n):
        @pl.when(found[j])
        def _():
            for h in range(2):
                copies(j, h, slots[j])[2].wait()


def add_arrived(group, arrived, own_of, codes, coarse):
    rows = codes.shape[0]
    owns, places = [], []
    for code in group:
        array, at = own_of[code]
        which = next((w for w, o in enumerate(owns) if o is array), len(owns))
        if which == len(owns):
            owns.append(array)
        places.append((which, at))
    n = len(group)
    m, b, _ = arrived[0].shape
    spec = pltpu.PrefetchScalarGridSpec(
        num_scalar_prefetch=1,
        grid=(1,),
        in_specs=[pl.BlockSpec(memory_space=pl.ANY)] * (n + len(owns) + 1),
        out_specs=pl.BlockSpec(memory_space=pl.ANY),
        scratch_shapes=[
            pltpu.VMEM((n, m, b, b), BF16),
            pltpu.VMEM((n, m, b, b), F32),
            pltpu.VMEM((n, m, b, b), BF16),
            pltpu.SemaphoreType.DMA((n, 2)),
            pltpu.SemaphoreType.DMA((n, 2)),
            pltpu.SemaphoreType.DMA((n, 2)),
        ],
    )
    return pl.pallas_call(
        functools.partial(add_kernel, group, places, rows, len(owns)),
        grid_spec=spec,
        out_shape=jax.ShapeDtypeStruct(coarse.shape, coarse.dtype),
        input_output_aliases={1 + n + len(owns): 0},
        cost_estimate=pl.CostEstimate(
            flops=n * m * b * b, bytes_accessed=n * m * b * b * 8, transcendentals=0
        ),
        name=f"add{n}",
    )(codes, *arrived, *owns, coarse)


def after(value, *others):
    return lax.optimization_barrier((value, *others))[0]


def local(blocks, prolong, cols, codes):
    groups, parts = lax.axis_size("grp"), lax.axis_size("mem")
    rows, width, b, _ = blocks.shape
    ks = tuple(k for k in range(width) if k != DIAG)
    place = lax.axis_index("grp").astype(jnp.int32).reshape(1)

    held, own_of = {}, {}

    def compute(group, gate):
        outs, own = terms(group, ks, gate, cols, blocks, prolong)
        for at, (code, out) in enumerate(zip(group, outs)):
            held[code], own_of[code] = out, (own, at)

    done = []

    def exchange(r):
        row = ROUNDS[r]
        moving = [held[code] for code in row]
        if r >= 2:
            moving = lax.optimization_barrier((moving, done[r - 2]))[0]
        got = [
            lax.ppermute(x, "grp", [(g, g ^ link) for g in range(groups)])
            for x, link in zip(moving, LINKS)
        ]
        done.append(got)
        for code, x in zip(row, got):
            held[code] = x

    compute(CALLS[0], codes)
    exchange(0)
    gate = after(codes, own_of[CALLS[0][0]][0])
    send, own_diag = diag_terms(groups, gate, place, blocks, prolong)
    came = lax.all_to_all(send, "grp", split_axis=0, concat_axis=0, tiled=True)
    gate = after(codes, own_diag)
    compute(CALLS[1], gate)
    exchange(1)
    gate = after(codes, own_of[CALLS[1][0]][0])
    compute(CALLS[2], gate)
    coarse, inv = inverses(parts, codes, place, own_diag, came, width)
    shared = lax.all_to_all(inv, "mem", split_axis=0, concat_axis=0, tiled=True)

    def finish(r, coarse):
        group = tuple(code for code in ROUNDS[r] if LAST[code] == r)
        if not group:
            return coarse
        return add_arrived(group, [held[code] for code in group], own_of, codes, coarse)

    for r in range(2, len(ROUNDS)):
        exchange(r)
        coarse = finish(r - 2, coarse)
    coarse = finish(len(ROUNDS) - 2, coarse)
    coarse = finish(len(ROUNDS) - 1, coarse)
    return coarse, shared.reshape(parts * rows, b // parts, b)


def solution(mesh):
    in_specs = (
        P(("grp", "mem"), None, None, None),
        P(("grp", "mem"), None, None),
        P(("grp", "mem"), None),
        P(("grp", "mem")),
    )
    out_specs = (P(("grp", "mem"), None, None, None), P("grp", "mem", None))
    return jax.shard_map(local, mesh=mesh, in_specs=in_specs, out_specs=out_specs, check_vma=False)
```

```python
import functools

import jax
import jax.numpy as jnp
from jax import lax
from jax.experimental import pallas as pl
from jax.experimental.pallas import tpu as pltpu
from jax.sharding import PartitionSpec as P


F32, BF16 = jnp.float32, jnp.bfloat16
DIAG = 13
HALF = 13
LINKS = (1, 3, 4, 12)
ROUNDS = (
    (5, 15, 7, 10),
    (9, 14, 6, 11),
    (10, 7, 5, 15),
    (2, 11, 8, 14),
    (6, 10, 9, 13),
    (14, 2, 11, 8),
    (13, 6, 10, 9),
)
CALLS = (ROUNDS[0], ROUNDS[1], (2, 8, 13))
LAST = {code: r for r, row in enumerate(ROUNDS) for code in row}


def pick(i, values):
    out = jnp.int32(values[0])
    for j, v in enumerate(values[1:], 1):
        out = jnp.where(i == j, jnp.int32(v), out)
    return out


def slot_of(codes_ref, code, rows):
    slot = jnp.int32(0)
    for s in range(rows):
        slot = jnp.where(codes_ref[s] == code, jnp.int32(s), slot)
    return slot


def has_code(codes_ref, code, rows):
    found = codes_ref[0] == code
    for s in range(1, rows):
        found = found | (codes_ref[s] == code)
    return found


def transposed(x):
    return x.astype(F32).T.astype(BF16)


def each_term(slot, ks, cols_ref, block_of, prolong_ref, use):
    left = transposed(prolong_ref[slot])
    for a in range(0, len(ks), 2):
        some = ks[a : a + 2]
        right = [
            jnp.dot(
                block_of(k), prolong_ref[cols_ref[slot, k]], preferred_element_type=F32
            ).astype(BF16)
            for k in some
        ]
        right = right[0] if len(right) == 1 else jnp.concatenate(right, axis=1)
        term = jnp.dot(left, right, preferred_element_type=F32)
        for b, k in enumerate(some):
            use(k, term[:, b * 128 : (b + 1) * 128])


def term_kernel(group, ks, pieces, rows, keep, codes_ref, cols_ref, blocks_ref, prolong_ref, *refs):
    n = len(group)
    outs, buf, sem = refs[: n * len(pieces)], refs[-2], refs[-1]
    owns = refs[n * len(pieces) : -2]
    i = pl.program_id(0)
    code = pick(i, group)
    slot = slot_of(codes_ref, code, rows)

    @pl.when(has_code(codes_ref, code, rows))
    def _():
        def use(k, term):
            at = ks.index(k)
            buf[i, at] = term.astype(BF16)
            if keep:
                owns[at // HALF][0, at % HALF] = term

        each_term(slot, ks, cols_ref, lambda k: blocks_ref[0, k - ks[0]], prolong_ref, use)

    def copies(j):
        for p, (at, count) in enumerate(pieces):
            yield pltpu.make_async_copy(
                buf.at[j, pl.ds(at, count)], outs[j * len(pieces) + p], sem.at[j, p]
            )

    for j in range(n):
        @pl.when(i == j)
        def _():
            for copy in copies(j):
                copy.start()

    @pl.when(i == n - 1)
    def _():
        for j in range(n):
            for copy in copies(j):
                copy.wait()


def terms(group, ks, pieces, codes, cols, blocks, prolong, keep=False):
    rows, _, b, _ = blocks.shape
    n, m, span = len(group), len(ks), ks[-1] + 1 - ks[0]
    spec = pltpu.PrefetchScalarGridSpec(
        num_scalar_prefetch=2,
        grid=(n,),
        in_specs=[
            pl.BlockSpec(
                (pl.Element(1), pl.Element(span), pl.Element(b), pl.Element(b)),
                lambda i, codes, cols: (slot_of(codes, pick(i, group), rows), ks[0], 0, 0),
            ),
            pl.BlockSpec((rows, b, b), lambda i, codes, cols: (0, 0, 0)),
        ],
        out_specs=[pl.BlockSpec(memory_space=pl.ANY)] * (n * len(pieces))
        + [pl.BlockSpec((1, HALF, b, b), lambda i, *_: (i, 0, 0, 0))] * (2 * keep),
        scratch_shapes=[
            pltpu.VMEM((n, m, b, b), BF16),
            pltpu.SemaphoreType.DMA((n, len(pieces))),
        ],
    )
    out = pl.pallas_call(
        functools.partial(term_kernel, group, ks, pieces, rows, keep),
        grid_spec=spec,
        out_shape=[jax.ShapeDtypeStruct((count, b, b), BF16) for _, count in pieces] * n
        + [jax.ShapeDtypeStruct((n, HALF, b, b), F32)] * (2 * keep),
        cost_estimate=pl.CostEstimate(
            flops=n * m * 4 * b**3, bytes_accessed=n * m * b * b * 4, transcendentals=0
        ),
    )(codes, cols, blocks, prolong)
    sent = [out[j * len(pieces) : (j + 1) * len(pieces)] for j in range(n)]
    return (sent, out[n * len(pieces) :]) if keep else sent


def diag_kernel(rows, codes_ref, place_ref, blocks_ref, prolong_ref, send_ref, own_ref):
    for s in range(rows):
        right = jnp.dot(blocks_ref[s, 0], prolong_ref[s], preferred_element_type=F32).astype(BF16)
        term = jnp.dot(transposed(prolong_ref[s]), right, preferred_element_type=F32)
        own_ref[s] = term
        send_ref[place_ref[0] ^ codes_ref[s]] = term.astype(BF16)


def diag_terms(groups, codes, place, blocks, prolong):
    rows, _, b, _ = blocks.shape
    spec = pltpu.PrefetchScalarGridSpec(
        num_scalar_prefetch=2,
        grid=(1,),
        in_specs=[
            pl.BlockSpec((rows, 1, b, b), lambda i, *_: (0, DIAG, 0, 0)),
            pl.BlockSpec((rows, b, b), lambda i, *_: (0, 0, 0)),
        ],
        out_specs=[
            pl.BlockSpec((groups, b, b), lambda i, *_: (0, 0, 0)),
            pl.BlockSpec((rows, b, b), lambda i, *_: (0, 0, 0)),
        ],
    )
    return pl.pallas_call(
        functools.partial(diag_kernel, rows),
        grid_spec=spec,
        out_shape=[
            jax.ShapeDtypeStruct((groups, b, b), BF16),
            jax.ShapeDtypeStruct((rows, b, b), F32),
        ],
        cost_estimate=pl.CostEstimate(
            flops=rows * 4 * b**3, bytes_accessed=rows * b * b * 10, transcendentals=0
        ),
        name="diag_terms",
    )(codes, place, blocks, prolong)


def inverse_kernel(rows, parts, codes_ref, place_ref, own_ref, arrived_ref, coarse_ref, inv_ref):
    b = own_ref.shape[1]
    share = b // parts
    row = lax.broadcasted_iota(jnp.int32, (b, b), 0)
    col = lax.broadcasted_iota(jnp.int32, (b, b), 1)
    on_diag = row == col
    two_eye = jnp.where(on_diag, 2.0, 0.0).astype(F32)
    dot = functools.partial(
        jnp.dot, precision=lax.Precision.HIGHEST, preferred_element_type=F32
    )
    for s in range(rows):
        d = own_ref[s] + arrived_ref[place_ref[0] ^ codes_ref[s]].astype(F32)
        coarse_ref[s, 0] = d.astype(BF16)
        only = jnp.where(on_diag, d, 0.0)
        by_col = 1.0 / jnp.sum(only, axis=0, keepdims=True)
        by_row = 1.0 / jnp.sum(only, axis=1, keepdims=True)
        x = by_row * (two_eye - d * by_col)
        x = dot(x, two_eye - dot(d, x))
        for j in range(parts):
            inv_ref[j, s] = x[j * share : (j + 1) * share]


def inverses(parts, codes, place, own, arrived, width):
    rows, b, _ = own.shape
    spec = pltpu.PrefetchScalarGridSpec(
        num_scalar_prefetch=2,
        grid=(1,),
        in_specs=[
            pl.BlockSpec(own.shape, lambda i, *_: (0, 0, 0)),
            pl.BlockSpec(arrived.shape, lambda i, *_: (0, 0, 0)),
        ],
        out_specs=[
            pl.BlockSpec((rows, 1, b, b), lambda i, *_: (0, DIAG, 0, 0)),
            pl.BlockSpec((parts, rows, b // parts, b), lambda i, *_: (0, 0, 0, 0)),
        ],
    )
    return pl.pallas_call(
        functools.partial(inverse_kernel, rows, parts),
        grid_spec=spec,
        out_shape=[
            jax.ShapeDtypeStruct((rows, width, b, b), BF16),
            jax.ShapeDtypeStruct((parts, rows, b // parts, b), F32),
        ],
        cost_estimate=pl.CostEstimate(
            flops=rows * 24 * b**3, bytes_accessed=rows * b * b * 12, transcendentals=0
        ),
        name="inverses",
    )(codes, place, own, arrived)


def add_kernel(group, ks, rows, codes_ref, cols_ref, prolong_ref, blocks_ref, *refs):
    n = len(group)
    arrived = refs[:n]
    coarse, buf_blocks, buf_out, sem_blocks, sem_out = refs[n + 1 :]
    lo, count = ks[0], ks[-1] + 1 - ks[0]
    slots = [slot_of(codes_ref, code, rows) for code in group]
    found = [has_code(codes_ref, code, rows) for code in group]
    runs = [(a, c) for a, c in ((0, DIAG), (DIAG + 1, HALF)) if a in ks]

    def take(j):
        return pltpu.make_async_copy(
            blocks_ref.at[slots[j], pl.ds(lo, count)], buf_blocks.at[j], sem_blocks.at[j]
        )

    def put(j):
        return [
            pltpu.make_async_copy(
                buf_out.at[j, pl.ds(a - lo, c)], coarse.at[slots[j], pl.ds(a, c)], sem_out.at[j, p]
            )
            for p, (a, c) in enumerate(runs)
        ]

    for j in range(n):
        @pl.when(found[j])
        def _():
            take(j).start()

    for j in range(n):
        @pl.when(found[j])
        def _():
            take(j).wait()

            def use(k, term):
                came = arrived[j][ks.index(k)].astype(F32)
                buf_out[j, k - lo] = (term + came).astype(BF16)

            each_term(
                slots[j],
                ks,
                cols_ref,
                lambda k: buf_blocks[j, k - lo],
                prolong_ref,
                use,
            )
            for copy in put(j):
                copy.start()

    for j in range(n):
        @pl.when(found[j])
        def _():
            for copy in put(j):
                copy.wait()


def add_arrived(group, ks, arrived, codes, cols, blocks, prolong, coarse):
    rows, _, b, _ = blocks.shape
    n, span = len(group), ks[-1] + 1 - ks[0]
    spec = pltpu.PrefetchScalarGridSpec(
        num_scalar_prefetch=2,
        grid=(1,),
        in_specs=[
            pl.BlockSpec((rows, b, b), lambda i, *_: (0, 0, 0)),
            pl.BlockSpec(memory_space=pl.ANY),
        ]
        + [pl.BlockSpec(memory_space=pltpu.VMEM)] * n
        + [pl.BlockSpec(memory_space=pl.ANY)],
        out_specs=pl.BlockSpec(memory_space=pl.ANY),
        scratch_shapes=[
            pltpu.VMEM((n, span, b, b), BF16),
            pltpu.VMEM((n, span, b, b), BF16),
            pltpu.SemaphoreType.DMA((n,)),
            pltpu.SemaphoreType.DMA((n, 2)),
        ],
    )
    return pl.pallas_call(
        functools.partial(add_kernel, group, ks, rows),
        grid_spec=spec,
        out_shape=jax.ShapeDtypeStruct(blocks.shape, BF16),
        input_output_aliases={4 + n: 0},
        cost_estimate=pl.CostEstimate(
            flops=n * len(ks) * 4 * b**3, bytes_accessed=n * span * b * b * 6, transcendentals=0
        ),
    )(codes, cols, prolong, blocks, *arrived, coarse)


def sum_kernel(group, at, rows, codes_ref, own_ref, *refs):
    n = len(group)
    arrived, (coarse, buf, sem) = refs[:n], refs[n + 1 :]
    count = buf.shape[1]
    slots = [slot_of(codes_ref, code, rows) for code in group]
    found = [has_code(codes_ref, code, rows) for code in group]

    def put(j):
        return pltpu.make_async_copy(
            buf.at[j], coarse.at[slots[j], pl.ds(at, count)], sem.at[j]
        )

    for j in range(n):
        @pl.when(found[j])
        def _():
            for k in range(count):
                buf[j, k] = (own_ref[j, k] + arrived[j][k].astype(F32)).astype(BF16)
            put(j).start()

    for j in range(n):
        @pl.when(found[j])
        def _():
            put(j).wait()


def sum_arrived(group, at, own, arrived, codes, coarse):
    rows = codes.shape[0]
    n, count, b, _ = own.shape
    spec = pltpu.PrefetchScalarGridSpec(
        num_scalar_prefetch=1,
        grid=(1,),
        in_specs=[pl.BlockSpec(memory_space=pltpu.VMEM)] * (n + 1)
        + [pl.BlockSpec(memory_space=pl.ANY)],
        out_specs=pl.BlockSpec(memory_space=pl.ANY),
        scratch_shapes=[pltpu.VMEM((n, count, b, b), BF16), pltpu.SemaphoreType.DMA((n,))],
    )
    return pl.pallas_call(
        functools.partial(sum_kernel, group, at, rows),
        grid_spec=spec,
        out_shape=jax.ShapeDtypeStruct(coarse.shape, BF16),
        input_output_aliases={2 + n: 0},
        cost_estimate=pl.CostEstimate(
            flops=n * count * b * b, bytes_accessed=n * count * b * b * 8, transcendentals=0
        ),
    )(codes, own, *arrived, coarse)


def copy_kernel(x_ref, o_ref):
    o_ref[...] = x_ref[...]


def after(value, *others):
    return lax.optimization_barrier((value, *others))[0]


def send(x, link, groups):
    return lax.ppermute(x, "grp", [(g, g ^ link) for g in range(groups)])


def local(blocks, prolong, cols, codes):
    groups, parts = lax.axis_size("grp"), lax.axis_size("mem")
    rows, width, b, _ = blocks.shape
    low, high = tuple(range(DIAG)), tuple(range(DIAG + 1, width))
    off = low + high
    total = len(off)

    held, done = {}, []

    def exchange(r, *ready):
        row = ROUNDS[r]
        moving = [held[code] for code in row]
        if r >= 2:
            moving, ready = lax.optimization_barrier((moving, (done[r - 2], *ready)))
            ready = ready[1:]
        got = [send(x, link, groups) for x, link in zip(moving, LINKS)]
        done.append(got)
        held.update(zip(row, got))
        return ready

    def finish(r, codes, coarse):
        group = tuple(code for code in ROUNDS[r] if LAST[code] == r)
        arrived = [held[code] for code in group]
        return add_arrived(group, off, arrived, codes, cols, blocks, prolong, coarse)

    place = lax.axis_index("grp").astype(jnp.int32).reshape(1)
    gate = codes
    for r in range(2):
        got = terms(CALLS[r], off, ((0, total),), gate, cols, blocks, prolong)
        held.update((code, x[0]) for code, x in zip(CALLS[r], got))
        exchange(r)
        gate = after(codes, got[0][0])
    table, own = diag_terms(groups, gate, place, blocks, prolong)
    table = lax.all_to_all(table, "grp", split_axis=0, concat_axis=0, tiled=True)
    gate = after(codes, own)
    got = terms(CALLS[2], off, ((0, total),), gate, cols, blocks, prolong)
    held.update((code, x[0]) for code, x in zip(CALLS[2], got))
    gate = after(codes, got[0][0])
    halves = ((0, HALF), (HALF, HALF))
    direct, kept = terms(LINKS, off, halves, gate, cols, blocks, prolong, True)

    for r in range(2, 7):
        exchange(r)
    coarse, inv = inverses(parts, codes, place, own, table, width)
    shared = lax.all_to_all(inv, "mem", split_axis=0, concat_axis=0, tiled=True)
    coarse = finish(2, codes, coarse)
    shared = pl.pallas_call(
        copy_kernel,
        in_specs=[pl.BlockSpec(memory_space=pltpu.VMEM)],
        out_shape=jax.ShapeDtypeStruct(shared.shape, F32),
        name="keep",
    )(shared)
    highs, _, coarse = lax.optimization_barrier(([x[1] for x in direct], done[5], coarse))
    lows = [send(x[0], link, groups) for x, link in zip(direct, LINKS)]
    highs = [send(x, link, groups) for x, link in zip(highs, LINKS)]
    coarse = finish(5, codes, coarse)
    coarse = finish(6, after(codes, shared), coarse)
    coarse = sum_arrived(LINKS, 0, kept[0], lows, codes, coarse)
    coarse = sum_arrived(LINKS, DIAG + 1, kept[1], highs, codes, coarse)
    return coarse, shared.reshape(parts * rows, b // parts, b)


def solution(mesh):
    in_specs = (
        P(("grp", "mem"), None, None, None),
        P(("grp", "mem"), None, None),
        P(("grp", "mem"), None),
        P(("grp", "mem")),
    )
    out_specs = (P(("grp", "mem"), None, None, None), P("grp", "mem", None))
    return jax.shard_map(local, mesh=mesh, in_specs=in_specs, out_specs=out_specs, check_vma=False)
```

```python
import functools

import jax
import jax.numpy as jnp
from jax import lax
from jax.experimental import pallas as pl
from jax.experimental.pallas import tpu as pltpu
from jax.sharding import PartitionSpec as P


F32, BF16 = jnp.float32, jnp.bfloat16
PARAMS = pltpu.CompilerParams(vmem_limit_bytes=36 * 2**20)
DIAG = 13
HALF = 13
LINKS = (1, 3, 4, 12)
ROUNDS = (
    (5, 15, 7, 10),
    (9, 14, 6, 11),
    (10, 7, 5, 15),
    (2, 11, 8, 14),
    (6, 10, 9, 13),
    (14, 2, 11, 8),
    (13, 6, 10, 9),
)
CALLS = (ROUNDS[0], ROUNDS[1], (2, 8, 13))
LAST = {code: r for r, row in enumerate(ROUNDS) for code in row}


def pick(i, values):
    out = jnp.int32(values[0])
    for j, v in enumerate(values[1:], 1):
        out = jnp.where(i == j, jnp.int32(v), out)
    return out


def slot_of(codes_ref, code, rows):
    slot = jnp.int32(0)
    for s in range(rows):
        slot = jnp.where(codes_ref[s] == code, jnp.int32(s), slot)
    return slot


def has_code(codes_ref, code, rows):
    found = codes_ref[0] == code
    for s in range(1, rows):
        found = found | (codes_ref[s] == code)
    return found


def transposed(x):
    return x.astype(F32).T.astype(BF16)


def each_term(slot, ks, cols_ref, block_of, prolong_ref, use):
    left = transposed(prolong_ref[slot])
    for a in range(0, len(ks), 2):
        some = ks[a : a + 2]
        right = [
            jnp.dot(
                block_of(k), prolong_ref[cols_ref[slot, k]], preferred_element_type=F32
            ).astype(BF16)
            for k in some
        ]
        right = right[0] if len(right) == 1 else jnp.concatenate(right, axis=1)
        term = jnp.dot(left, right, preferred_element_type=F32)
        for b, k in enumerate(some):
            use(k, term[:, b * 128 : (b + 1) * 128])


def term_kernel(group, ks, pieces, rows, keep, codes_ref, cols_ref, blocks_ref, prolong_ref, *refs):
    n = len(group)
    outs, buf, sem = refs[: n * len(pieces)], refs[-2], refs[-1]
    owns = refs[n * len(pieces) : -2]
    i = pl.program_id(0)
    code = pick(i, group)
    slot = slot_of(codes_ref, code, rows)

    @pl.when(has_code(codes_ref, code, rows))
    def _():
        def use(k, term):
            at = ks.index(k)
            buf[i, at] = term.astype(BF16)
            if keep:
                owns[at // HALF][0, at % HALF] = term

        each_term(slot, ks, cols_ref, lambda k: blocks_ref[0, k - ks[0]], prolong_ref, use)

    def copies(j):
        for p, (at, count) in enumerate(pieces):
            yield pltpu.make_async_copy(
                buf.at[j, pl.ds(at, count)], outs[j * len(pieces) + p], sem.at[j, p]
            )

    for j in range(n):
        @pl.when(i == j)
        def _():
            for copy in copies(j):
                copy.start()

    @pl.when(i == n - 1)
    def _():
        for j in range(n):
            for copy in copies(j):
                copy.wait()


def terms(group, ks, pieces, codes, cols, blocks, prolong, keep=False):
    rows, _, b, _ = blocks.shape
    n, m, span = len(group), len(ks), ks[-1] + 1 - ks[0]
    spec = pltpu.PrefetchScalarGridSpec(
        num_scalar_prefetch=2,
        grid=(n,),
        in_specs=[
            pl.BlockSpec(
                (pl.Element(1), pl.Element(span), pl.Element(b), pl.Element(b)),
                lambda i, codes, cols: (slot_of(codes, pick(i, group), rows), ks[0], 0, 0),
            ),
            pl.BlockSpec((rows, b, b), lambda i, codes, cols: (0, 0, 0)),
        ],
        out_specs=[pl.BlockSpec(memory_space=pl.ANY)] * (n * len(pieces))
        + [pl.BlockSpec((1, HALF, b, b), lambda i, *_: (i, 0, 0, 0))] * (2 * keep),
        scratch_shapes=[
            pltpu.VMEM((n, m, b, b), BF16),
            pltpu.SemaphoreType.DMA((n, len(pieces))),
        ],
    )
    out = pl.pallas_call(
        functools.partial(term_kernel, group, ks, pieces, rows, keep),
        grid_spec=spec,
        out_shape=[jax.ShapeDtypeStruct((count, b, b), BF16) for _, count in pieces] * n
        + [jax.ShapeDtypeStruct((n, HALF, b, b), F32)] * (2 * keep),
        cost_estimate=pl.CostEstimate(
            flops=n * m * 4 * b**3, bytes_accessed=n * m * b * b * 4, transcendentals=0
        ),
    )(codes, cols, blocks, prolong)
    sent = [out[j * len(pieces) : (j + 1) * len(pieces)] for j in range(n)]
    return (sent, out[n * len(pieces) :]) if keep else sent


def diag_kernel(rows, codes_ref, place_ref, blocks_ref, prolong_ref, send_ref, own_ref):
    for s in range(rows):
        right = jnp.dot(blocks_ref[s, 0], prolong_ref[s], preferred_element_type=F32).astype(BF16)
        term = jnp.dot(transposed(prolong_ref[s]), right, preferred_element_type=F32)
        own_ref[s] = term
        send_ref[place_ref[0] ^ codes_ref[s]] = term.astype(BF16)


def diag_terms(groups, codes, place, blocks, prolong):
    rows, _, b, _ = blocks.shape
    spec = pltpu.PrefetchScalarGridSpec(
        num_scalar_prefetch=2,
        grid=(1,),
        in_specs=[
            pl.BlockSpec((rows, 1, b, b), lambda i, *_: (0, DIAG, 0, 0)),
            pl.BlockSpec((rows, b, b), lambda i, *_: (0, 0, 0)),
        ],
        out_specs=[
            pl.BlockSpec((groups, b, b), lambda i, *_: (0, 0, 0)),
            pl.BlockSpec((rows, b, b), lambda i, *_: (0, 0, 0)),
        ],
    )
    return pl.pallas_call(
        functools.partial(diag_kernel, rows),
        grid_spec=spec,
        out_shape=[
            jax.ShapeDtypeStruct((groups, b, b), BF16),
            jax.ShapeDtypeStruct((rows, b, b), F32),
        ],
        cost_estimate=pl.CostEstimate(
            flops=rows * 4 * b**3, bytes_accessed=rows * b * b * 10, transcendentals=0
        ),
        name="diag_terms",
    )(codes, place, blocks, prolong)


def inverse_kernel(rows, parts, codes_ref, place_ref, own_ref, arrived_ref, coarse_ref, inv_ref):
    b = own_ref.shape[1]
    share = b // parts
    row = lax.broadcasted_iota(jnp.int32, (b, b), 0)
    col = lax.broadcasted_iota(jnp.int32, (b, b), 1)
    on_diag = row == col
    two_eye = jnp.where(on_diag, 2.0, 0.0).astype(F32)
    dot = functools.partial(
        jnp.dot, precision=lax.Precision.HIGHEST, preferred_element_type=F32
    )
    for s in range(rows):
        d = own_ref[s] + arrived_ref[place_ref[0] ^ codes_ref[s]].astype(F32)
        coarse_ref[s, 0] = d.astype(BF16)
        only = jnp.where(on_diag, d, 0.0)
        by_col = 1.0 / jnp.sum(only, axis=0, keepdims=True)
        by_row = 1.0 / jnp.sum(only, axis=1, keepdims=True)
        x = by_row * (two_eye - d * by_col)
        x = dot(x, two_eye - dot(d, x))
        for j in range(parts):
            inv_ref[j, s] = x[j * share : (j + 1) * share]


def inverses(parts, codes, place, own, arrived, width):
    rows, b, _ = own.shape
    spec = pltpu.PrefetchScalarGridSpec(
        num_scalar_prefetch=2,
        grid=(1,),
        in_specs=[
            pl.BlockSpec(own.shape, lambda i, *_: (0, 0, 0)),
            pl.BlockSpec(arrived.shape, lambda i, *_: (0, 0, 0)),
        ],
        out_specs=[
            pl.BlockSpec((rows, 1, b, b), lambda i, *_: (0, DIAG, 0, 0)),
            pl.BlockSpec((parts, rows, b // parts, b), lambda i, *_: (0, 0, 0, 0)),
        ],
    )
    return pl.pallas_call(
        functools.partial(inverse_kernel, rows, parts),
        grid_spec=spec,
        out_shape=[
            jax.ShapeDtypeStruct((rows, width, b, b), BF16),
            jax.ShapeDtypeStruct((parts, rows, b // parts, b), F32),
        ],
        cost_estimate=pl.CostEstimate(
            flops=rows * 24 * b**3, bytes_accessed=rows * b * b * 12, transcendentals=0
        ),
        name="inverses",
    )(codes, place, own, arrived)


def add_kernel(group, ks, rows, codes_ref, cols_ref, prolong_ref, blocks_ref, *refs):
    n = len(group)
    arrived = refs[:n]
    coarse, buf_blocks, buf_out, sem_blocks, sem_out = refs[n + 1 :]
    lo, count = ks[0], ks[-1] + 1 - ks[0]
    slots = [slot_of(codes_ref, code, rows) for code in group]
    found = [has_code(codes_ref, code, rows) for code in group]
    runs = [(a, c) for a, c in ((0, DIAG), (DIAG + 1, HALF)) if a in ks]

    def take(j):
        return pltpu.make_async_copy(
            blocks_ref.at[slots[j], pl.ds(lo, count)], buf_blocks.at[j], sem_blocks.at[j]
        )

    def put(j):
        return [
            pltpu.make_async_copy(
                buf_out.at[j, pl.ds(a - lo, c)], coarse.at[slots[j], pl.ds(a, c)], sem_out.at[j, p]
            )
            for p, (a, c) in enumerate(runs)
        ]

    for j in range(n):
        @pl.when(found[j])
        def _():
            take(j).start()

    for j in range(n):
        @pl.when(found[j])
        def _():
            take(j).wait()

            def use(k, term):
                came = arrived[j][ks.index(k)].astype(F32)
                buf_out[j, k - lo] = (term + came).astype(BF16)

            each_term(
                slots[j],
                ks,
                cols_ref,
                lambda k: buf_blocks[j, k - lo],
                prolong_ref,
                use,
            )
            for copy in put(j):
                copy.start()

    for j in range(n):
        @pl.when(found[j])
        def _():
            for copy in put(j):
                copy.wait()


def add_arrived(group, ks, arrived, codes, cols, blocks, prolong, coarse, at_hand):
    rows, _, b, _ = blocks.shape
    n, span = len(group), ks[-1] + 1 - ks[0]
    spec = pltpu.PrefetchScalarGridSpec(
        num_scalar_prefetch=2,
        grid=(1,),
        in_specs=[
            pl.BlockSpec((rows, b, b), lambda i, *_: (0, 0, 0)),
            pl.BlockSpec(memory_space=pl.ANY),
        ]
        + [pl.BlockSpec(memory_space=pltpu.VMEM)] * n
        + [pl.BlockSpec(memory_space=pl.ANY)],
        out_specs=pl.BlockSpec(memory_space=pl.ANY),
        scratch_shapes=[
            pltpu.VMEM((n, span, b, b), BF16),
            pltpu.VMEM((n, span, b, b), BF16),
            pltpu.SemaphoreType.DMA((n,)),
            pltpu.SemaphoreType.DMA((n, 2)),
        ],
    )
    return pl.pallas_call(
        functools.partial(add_kernel, group, ks, rows),
        grid_spec=spec,
        out_shape=jax.ShapeDtypeStruct(blocks.shape, BF16),
        input_output_aliases={4 + n: 0},
        compiler_params=PARAMS,
        cost_estimate=pl.CostEstimate(
            flops=n * len(ks) * 4 * b**3, bytes_accessed=n * span * b * b * 6, transcendentals=0
        ),
    )(
        far(codes),
        far(cols),
        far(prolong),
        far(blocks),
        *(near(x) if at_hand else x for x in arrived),
        far(coarse),
    )


def sum_kernel(group, at, rows, codes_ref, own_ref, *refs):
    n = len(group)
    arrived, (coarse, buf, sem) = refs[:n], refs[n + 1 :]
    count = buf.shape[1]
    slots = [slot_of(codes_ref, code, rows) for code in group]
    found = [has_code(codes_ref, code, rows) for code in group]

    def put(j):
        return pltpu.make_async_copy(
            buf.at[j], coarse.at[slots[j], pl.ds(at, count)], sem.at[j]
        )

    for j in range(n):
        @pl.when(found[j])
        def _():
            for k in range(count):
                buf[j, k] = (own_ref[j, k] + arrived[j][k].astype(F32)).astype(BF16)
            put(j).start()

    for j in range(n):
        @pl.when(found[j])
        def _():
            put(j).wait()


def sum_arrived(group, at, own, arrived, codes, coarse):
    rows = codes.shape[0]
    n, count, b, _ = own.shape
    spec = pltpu.PrefetchScalarGridSpec(
        num_scalar_prefetch=1,
        grid=(1,),
        in_specs=[pl.BlockSpec(memory_space=pltpu.VMEM)] * (n + 1)
        + [pl.BlockSpec(memory_space=pl.ANY)],
        out_specs=pl.BlockSpec(memory_space=pl.ANY),
        scratch_shapes=[pltpu.VMEM((n, count, b, b), BF16), pltpu.SemaphoreType.DMA((n,))],
    )
    return pl.pallas_call(
        functools.partial(sum_kernel, group, at, rows),
        grid_spec=spec,
        out_shape=jax.ShapeDtypeStruct(coarse.shape, BF16),
        input_output_aliases={2 + n: 0},
        compiler_params=PARAMS,
        cost_estimate=pl.CostEstimate(
            flops=n * count * b * b, bytes_accessed=n * count * b * b * 8, transcendentals=0
        ),
    )(far(codes), near(own), *map(near, arrived), far(coarse))


def copy_kernel(x_ref, o_ref):
    o_ref[...] = x_ref[...]


def near(x):
    return pltpu.with_memory_space_constraint(x, pltpu.VMEM)


def far(x):
    return pltpu.with_memory_space_constraint(x, pltpu.HBM)


def after(value, *others):
    return lax.optimization_barrier((value, *others))[0]


def send(x, link, groups):
    return lax.ppermute(x, "grp", [(g, g ^ link) for g in range(groups)])


def local(blocks, prolong, cols, codes):
    groups, parts = lax.axis_size("grp"), lax.axis_size("mem")
    rows, width, b, _ = blocks.shape
    low, high = tuple(range(DIAG)), tuple(range(DIAG + 1, width))
    off = low + high
    total = len(off)

    held, done = {}, []

    def exchange(r, *ready):
        row = ROUNDS[r]
        moving = [held[code] for code in row]
        if r >= 2:
            moving, ready = lax.optimization_barrier((moving, (done[r - 2], *ready)))
            ready = ready[1:]
        got = [send(x, link, groups) for x, link in zip(moving, LINKS)]
        done.append(got)
        held.update(zip(row, got))
        return ready

    def finish(r, codes, coarse):
        group = tuple(code for code in ROUNDS[r] if LAST[code] == r)
        arrived = [held[code] for code in group]
        return add_arrived(group, off, arrived, codes, cols, blocks, prolong, coarse, r > 2)

    place = lax.axis_index("grp").astype(jnp.int32).reshape(1)
    gate = codes
    for r in range(2):
        got = terms(CALLS[r], off, ((0, total),), gate, cols, blocks, prolong)
        held.update((code, x[0]) for code, x in zip(CALLS[r], got))
        exchange(r)
        gate = after(codes, got[0][0])
    table, own = diag_terms(groups, gate, place, blocks, prolong)
    table = lax.all_to_all(table, "grp", split_axis=0, concat_axis=0, tiled=True)
    gate = after(codes, own)
    got = terms(CALLS[2], off, ((0, total),), gate, cols, blocks, prolong)
    held.update((code, x[0]) for code, x in zip(CALLS[2], got))
    gate = after(codes, got[0][0])
    halves = ((0, HALF), (HALF, HALF))
    direct, kept = terms(LINKS, off, halves, gate, cols, blocks, prolong, True)

    for r in range(2, 7):
        exchange(r)
    coarse, inv = inverses(parts, codes, place, own, table, width)
    shared = lax.all_to_all(inv, "mem", split_axis=0, concat_axis=0, tiled=True)
    coarse = finish(2, codes, coarse)
    shared = pl.pallas_call(
        copy_kernel,
        in_specs=[pl.BlockSpec(memory_space=pltpu.VMEM)],
        out_shape=jax.ShapeDtypeStruct(shared.shape, F32),
        name="keep",
    )(near(shared))
    highs, _, coarse = lax.optimization_barrier(([x[1] for x in direct], done[5], coarse))
    lows = [send(x[0], link, groups) for x, link in zip(direct, LINKS)]
    highs = [send(x, link, groups) for x, link in zip(highs, LINKS)]
    coarse = finish(5, codes, coarse)
    coarse = finish(6, after(codes, shared), coarse)
    coarse = sum_arrived(LINKS, 0, kept[0], lows, codes, coarse)
    coarse = sum_arrived(LINKS, DIAG + 1, kept[1], highs, codes, coarse)
    return coarse, shared.reshape(parts * rows, b // parts, b)


def solution(mesh):
    in_specs = (
        P(("grp", "mem"), None, None, None),
        P(("grp", "mem"), None, None),
        P(("grp", "mem"), None),
        P(("grp", "mem")),
    )
    out_specs = (P(("grp", "mem"), None, None, None), P("grp", "mem", None))
    return jax.shard_map(local, mesh=mesh, in_specs=in_specs, out_specs=out_specs, check_vma=False)
```

```python
import functools

import jax
import jax.numpy as jnp
from jax import lax
from jax.experimental import pallas as pl
from jax.experimental.pallas import tpu as pltpu
from jax.sharding import PartitionSpec as P


F32, BF16 = jnp.float32, jnp.bfloat16
PARAMS = pltpu.CompilerParams(vmem_limit_bytes=36 * 2**20)
DIAG = 13
HALF = 13
LINKS = (1, 3, 4, 12)
ROUNDS = (
    (5, 15, 7, 10),
    (9, 14, 6, 11),
    (10, 7, 5, 15),
    (2, 11, 8, 14),
    (6, 10, 9, 13),
    (14, 2, 11, 8),
    (13, 6, 10, 9),
)
CALLS = (ROUNDS[0], ROUNDS[1], (2, 8, 13))
LAST = {code: r for r, row in enumerate(ROUNDS) for code in row}


def pick(i, values):
    out = jnp.int32(values[0])
    for j, v in enumerate(values[1:], 1):
        out = jnp.where(i == j, jnp.int32(v), out)
    return out


def slot_of(codes_ref, code, rows):
    slot = jnp.int32(0)
    for s in range(rows):
        slot = jnp.where(codes_ref[s] == code, jnp.int32(s), slot)
    return slot


def has_code(codes_ref, code, rows):
    found = codes_ref[0] == code
    for s in range(1, rows):
        found = found | (codes_ref[s] == code)
    return found


def transposed(x):
    return x.astype(F32).T.astype(BF16)


def each_term(slot, ks, cols_ref, block_of, prolong_ref, use):
    left = transposed(prolong_ref[slot])
    for a in range(0, len(ks), 2):
        some = ks[a : a + 2]
        right = [
            jnp.dot(
                block_of(k), prolong_ref[cols_ref[slot, k]], preferred_element_type=F32
            ).astype(BF16)
            for k in some
        ]
        right = right[0] if len(right) == 1 else jnp.concatenate(right, axis=1)
        term = jnp.dot(left, right, preferred_element_type=F32)
        for b, k in enumerate(some):
            use(k, term[:, b * 128 : (b + 1) * 128])


def term_kernel(group, ks, pieces, rows, keep, codes_ref, cols_ref, blocks_ref, prolong_ref, *refs):
    n = len(group)
    outs, buf, sem = refs[: n * len(pieces)], refs[-2], refs[-1]
    owns = refs[n * len(pieces) : -2]
    i = pl.program_id(0)
    code = pick(i, group)
    slot = slot_of(codes_ref, code, rows)

    @pl.when(has_code(codes_ref, code, rows))
    def _():
        def use(k, term):
            at = ks.index(k)
            buf[i, at] = term.astype(BF16)
            if keep:
                owns[0][0, at] = term

        each_term(slot, ks, cols_ref, lambda k: blocks_ref[0, k - ks[0]], prolong_ref, use)

    def copies(j):
        for p, (at, count) in enumerate(pieces):
            yield pltpu.make_async_copy(
                buf.at[j, pl.ds(at, count)], outs[j * len(pieces) + p], sem.at[j, p]
            )

    for j in range(n):
        @pl.when(i == j)
        def _():
            for copy in copies(j):
                copy.start()

    @pl.when(i == n - 1)
    def _():
        for j in range(n):
            for copy in copies(j):
                copy.wait()


def terms(group, ks, pieces, codes, cols, blocks, prolong, keep=False):
    rows, _, b, _ = blocks.shape
    n, m, span = len(group), len(ks), ks[-1] + 1 - ks[0]
    spec = pltpu.PrefetchScalarGridSpec(
        num_scalar_prefetch=2,
        grid=(n,),
        in_specs=[
            pl.BlockSpec(
                (pl.Element(1), pl.Element(span), pl.Element(b), pl.Element(b)),
                lambda i, codes, cols: (slot_of(codes, pick(i, group), rows), ks[0], 0, 0),
            ),
            pl.BlockSpec((rows, b, b), lambda i, codes, cols: (0, 0, 0)),
        ],
        out_specs=[pl.BlockSpec(memory_space=pl.ANY)] * (n * len(pieces))
        + [pl.BlockSpec((1, m, b, b), lambda i, *_: (i, 0, 0, 0))] * keep,
        scratch_shapes=[
            pltpu.VMEM((n, m, b, b), BF16),
            pltpu.SemaphoreType.DMA((n, len(pieces))),
        ],
    )
    out = pl.pallas_call(
        functools.partial(term_kernel, group, ks, pieces, rows, keep),
        grid_spec=spec,
        out_shape=[jax.ShapeDtypeStruct((count, b, b), BF16) for _, count in pieces] * n
        + [jax.ShapeDtypeStruct((n, m, b, b), F32)] * keep,
        cost_estimate=pl.CostEstimate(
            flops=n * m * 4 * b**3, bytes_accessed=n * m * b * b * 4, transcendentals=0
        ),
    )(codes, cols, blocks, prolong)
    sent = [out[j * len(pieces) : (j + 1) * len(pieces)] for j in range(n)]
    return (sent, out[n * len(pieces) :]) if keep else sent


def diag_kernel(rows, codes_ref, place_ref, blocks_ref, prolong_ref, send_ref, own_ref):
    for s in range(rows):
        right = jnp.dot(blocks_ref[s, 0], prolong_ref[s], preferred_element_type=F32).astype(BF16)
        term = jnp.dot(transposed(prolong_ref[s]), right, preferred_element_type=F32)
        own_ref[s] = term
        send_ref[place_ref[0] ^ codes_ref[s]] = term.astype(BF16)


def diag_terms(groups, codes, place, blocks, prolong):
    rows, _, b, _ = blocks.shape
    spec = pltpu.PrefetchScalarGridSpec(
        num_scalar_prefetch=2,
        grid=(1,),
        in_specs=[
            pl.BlockSpec((rows, 1, b, b), lambda i, *_: (0, DIAG, 0, 0)),
            pl.BlockSpec((rows, b, b), lambda i, *_: (0, 0, 0)),
        ],
        out_specs=[
            pl.BlockSpec((groups, b, b), lambda i, *_: (0, 0, 0)),
            pl.BlockSpec((rows, b, b), lambda i, *_: (0, 0, 0)),
        ],
    )
    return pl.pallas_call(
        functools.partial(diag_kernel, rows),
        grid_spec=spec,
        out_shape=[
            jax.ShapeDtypeStruct((groups, b, b), BF16),
            jax.ShapeDtypeStruct((rows, b, b), F32),
        ],
        cost_estimate=pl.CostEstimate(
            flops=rows * 4 * b**3, bytes_accessed=rows * b * b * 10, transcendentals=0
        ),
        name="diag_terms",
    )(codes, place, blocks, prolong)


def inverse_kernel(rows, parts, codes_ref, place_ref, own_ref, arrived_ref, coarse_ref, inv_ref):
    b = own_ref.shape[1]
    share = b // parts
    row = lax.broadcasted_iota(jnp.int32, (b, b), 0)
    col = lax.broadcasted_iota(jnp.int32, (b, b), 1)
    on_diag = row == col
    two_eye = jnp.where(on_diag, 2.0, 0.0).astype(F32)
    dot = functools.partial(
        jnp.dot, precision=lax.Precision.HIGHEST, preferred_element_type=F32
    )
    for s in range(rows):
        d = own_ref[s] + arrived_ref[place_ref[0] ^ codes_ref[s]].astype(F32)
        coarse_ref[s, 0] = d.astype(BF16)
        only = jnp.where(on_diag, d, 0.0)
        by_col = 1.0 / jnp.sum(only, axis=0, keepdims=True)
        by_row = 1.0 / jnp.sum(only, axis=1, keepdims=True)
        x = by_row * (two_eye - d * by_col)
        x = dot(x, two_eye - dot(d, x))
        for j in range(parts):
            inv_ref[j, s] = x[j * share : (j + 1) * share]


def inverses(parts, codes, place, own, arrived, width):
    rows, b, _ = own.shape
    spec = pltpu.PrefetchScalarGridSpec(
        num_scalar_prefetch=2,
        grid=(1,),
        in_specs=[
            pl.BlockSpec(own.shape, lambda i, *_: (0, 0, 0)),
            pl.BlockSpec(arrived.shape, lambda i, *_: (0, 0, 0)),
        ],
        out_specs=[
            pl.BlockSpec((rows, 1, b, b), lambda i, *_: (0, DIAG, 0, 0)),
            pl.BlockSpec((parts, rows, b // parts, b), lambda i, *_: (0, 0, 0, 0)),
        ],
    )
    return pl.pallas_call(
        functools.partial(inverse_kernel, rows, parts),
        grid_spec=spec,
        out_shape=[
            jax.ShapeDtypeStruct((rows, width, b, b), BF16),
            jax.ShapeDtypeStruct((parts, rows, b // parts, b), F32),
        ],
        cost_estimate=pl.CostEstimate(
            flops=rows * 24 * b**3, bytes_accessed=rows * b * b * 12, transcendentals=0
        ),
        name="inverses",
    )(codes, place, own, arrived)


def add_kernel(group, ks, rows, codes_ref, cols_ref, prolong_ref, blocks_ref, *refs):
    n = len(group)
    arrived = refs[:n]
    coarse, buf_blocks, buf_out, sem_blocks, sem_out = refs[n + 1 :]
    lo, count = ks[0], ks[-1] + 1 - ks[0]
    slots = [slot_of(codes_ref, code, rows) for code in group]
    found = [has_code(codes_ref, code, rows) for code in group]
    runs = [(a, c) for a, c in ((0, DIAG), (DIAG + 1, HALF)) if a in ks]

    def take(j):
        return pltpu.make_async_copy(
            blocks_ref.at[slots[j], pl.ds(lo, count)], buf_blocks.at[j], sem_blocks.at[j]
        )

    def put(j):
        return [
            pltpu.make_async_copy(
                buf_out.at[j, pl.ds(a - lo, c)], coarse.at[slots[j], pl.ds(a, c)], sem_out.at[j, p]
            )
            for p, (a, c) in enumerate(runs)
        ]

    for j in range(n):
        @pl.when(found[j])
        def _():
            take(j).start()

    for j in range(n):
        @pl.when(found[j])
        def _():
            take(j).wait()

            def use(k, term):
                came = arrived[j][ks.index(k)].astype(F32)
                buf_out[j, k - lo] = (term + came).astype(BF16)

            each_term(
                slots[j],
                ks,
                cols_ref,
                lambda k: buf_blocks[j, k - lo],
                prolong_ref,
                use,
            )
            for copy in put(j):
                copy.start()

    for j in range(n):
        @pl.when(found[j])
        def _():
            for copy in put(j):
                copy.wait()


def add_arrived(group, ks, arrived, codes, cols, blocks, prolong, coarse, at_hand):
    rows, _, b, _ = blocks.shape
    n, span = len(group), ks[-1] + 1 - ks[0]
    spec = pltpu.PrefetchScalarGridSpec(
        num_scalar_prefetch=2,
        grid=(1,),
        in_specs=[
            pl.BlockSpec((rows, b, b), lambda i, *_: (0, 0, 0)),
            pl.BlockSpec(memory_space=pl.ANY),
        ]
        + [pl.BlockSpec(memory_space=pltpu.VMEM)] * n
        + [pl.BlockSpec(memory_space=pl.ANY)],
        out_specs=pl.BlockSpec(memory_space=pl.ANY),
        scratch_shapes=[
            pltpu.VMEM((n, span, b, b), BF16),
            pltpu.VMEM((n, span, b, b), BF16),
            pltpu.SemaphoreType.DMA((n,)),
            pltpu.SemaphoreType.DMA((n, 2)),
        ],
    )
    return pl.pallas_call(
        functools.partial(add_kernel, group, ks, rows),
        grid_spec=spec,
        out_shape=jax.ShapeDtypeStruct(blocks.shape, BF16),
        input_output_aliases={4 + n: 0},
        compiler_params=PARAMS,
        cost_estimate=pl.CostEstimate(
            flops=n * len(ks) * 4 * b**3, bytes_accessed=n * span * b * b * 6, transcendentals=0
        ),
    )(
        far(codes),
        far(cols),
        far(prolong),
        far(blocks),
        *(near(x) if at_hand else x for x in arrived),
        far(coarse),
    )


def sum_kernel(group, runs, rows, codes_ref, own_ref, *refs):
    n = len(group)
    arrived, (coarse, buf, sem) = refs[:n], refs[n + 1 :]
    count = buf.shape[1]
    slots = [slot_of(codes_ref, code, rows) for code in group]
    found = [has_code(codes_ref, code, rows) for code in group]

    def put(j):
        return [
            pltpu.make_async_copy(
                buf.at[j, pl.ds(p * HALF, HALF)], coarse.at[slots[j], pl.ds(at, HALF)], sem.at[j, p]
            )
            for p, at in enumerate(runs)
        ]

    for j in range(n):
        @pl.when(found[j])
        def _():
            for k in range(count):
                buf[j, k] = (own_ref[j, k] + arrived[j][k].astype(F32)).astype(BF16)
                if k % HALF == HALF - 1:
                    put(j)[k // HALF].start()

    for j in range(n):
        @pl.when(found[j])
        def _():
            for copy in put(j):
                copy.wait()


def sum_arrived(group, runs, own, arrived, codes, coarse):
    rows = codes.shape[0]
    n, count, b, _ = own.shape
    spec = pltpu.PrefetchScalarGridSpec(
        num_scalar_prefetch=1,
        grid=(1,),
        in_specs=[pl.BlockSpec(memory_space=pltpu.VMEM)] * (n + 1)
        + [pl.BlockSpec(memory_space=pl.ANY)],
        out_specs=pl.BlockSpec(memory_space=pl.ANY),
        scratch_shapes=[
            pltpu.VMEM((n, count, b, b), BF16),
            pltpu.SemaphoreType.DMA((n, len(runs))),
        ],
    )
    return pl.pallas_call(
        functools.partial(sum_kernel, group, runs, rows),
        grid_spec=spec,
        out_shape=jax.ShapeDtypeStruct(coarse.shape, BF16),
        input_output_aliases={2 + n: 0},
        compiler_params=PARAMS,
        cost_estimate=pl.CostEstimate(
            flops=n * count * b * b, bytes_accessed=n * count * b * b * 8, transcendentals=0
        ),
    )(far(codes), near(own), *map(near, arrived), far(coarse))


def copy_kernel(x_ref, o_ref):
    o_ref[...] = x_ref[...]


def near(x):
    return pltpu.with_memory_space_constraint(x, pltpu.VMEM)


def far(x):
    return pltpu.with_memory_space_constraint(x, pltpu.HBM)


def after(value, *others):
    return lax.optimization_barrier((value, *others))[0]


def send(x, link, groups):
    return lax.ppermute(x, "grp", [(g, g ^ link) for g in range(groups)])


def local(blocks, prolong, cols, codes):
    groups, parts = lax.axis_size("grp"), lax.axis_size("mem")
    rows, width, b, _ = blocks.shape
    low, high = tuple(range(DIAG)), tuple(range(DIAG + 1, width))
    off = low + high
    total = len(off)

    held, done = {}, []

    def exchange(r, *ready):
        row = ROUNDS[r]
        moving = [held[code] for code in row]
        if r >= 2:
            moving, ready = lax.optimization_barrier((moving, (done[r - 2], *ready)))
            ready = ready[1:]
        got = [send(x, link, groups) for x, link in zip(moving, LINKS)]
        done.append(got)
        held.update(zip(row, got))
        return ready

    def finish(r, codes, coarse):
        group = tuple(code for code in ROUNDS[r] if LAST[code] == r)
        arrived = [held[code] for code in group]
        return add_arrived(group, off, arrived, codes, cols, blocks, prolong, coarse, False)

    place = lax.axis_index("grp").astype(jnp.int32).reshape(1)
    got = terms(LINKS, low, ((0, HALF),), codes, cols, blocks, prolong)
    gate = after(codes, got[0][0])
    lows = [send(x[0], link, groups) for x, link in zip(got, LINKS)]
    for r in range(2):
        got = terms(CALLS[r], off, ((0, total),), gate, cols, blocks, prolong)
        held.update((code, x[0]) for code, x in zip(CALLS[r], got))
        exchange(r)
        gate = after(codes, got[0][0])
    table, own = diag_terms(groups, gate, place, blocks, prolong)
    table = lax.all_to_all(table, "grp", split_axis=0, concat_axis=0, tiled=True)
    gate = after(codes, own)
    got = terms(CALLS[2], off, ((0, total),), gate, cols, blocks, prolong)
    held.update((code, x[0]) for code, x in zip(CALLS[2], got))
    gate = after(codes, got[0][0])
    highs, kept = terms(LINKS, high, ((0, HALF),), gate, cols, blocks, prolong, True)

    for r in range(2, 7):
        exchange(r)
    coarse, inv = inverses(parts, codes, place, own, table, width)
    shared = lax.all_to_all(inv, "mem", split_axis=0, concat_axis=0, tiled=True)
    coarse = add_arrived(LINKS, low, lows, codes, cols, blocks, prolong, coarse, False)
    coarse = finish(2, codes, coarse)
    _, (spare,) = terms(ROUNDS[6], off, ((0, 1),), codes, cols, blocks, prolong, True)
    shared = pl.pallas_call(
        copy_kernel,
        in_specs=[pl.BlockSpec(memory_space=pltpu.VMEM)],
        out_shape=jax.ShapeDtypeStruct(shared.shape, F32),
        name="keep",
    )(near(shared))
    highs, _, coarse = lax.optimization_barrier(([x[0] for x in highs], done[5], coarse))
    highs = [send(x, link, groups) for x, link in zip(highs, LINKS)]
    coarse = finish(5, codes, coarse)
    arrived = [held[code] for code in ROUNDS[6]]
    runs = (0, DIAG + 1)
    coarse = sum_arrived(ROUNDS[6], runs, spare, arrived, after(codes, shared), coarse)
    coarse = sum_arrived(LINKS, runs[1:], kept[0], highs, codes, coarse)
    return coarse, shared.reshape(parts * rows, b // parts, b)


def solution(mesh):
    in_specs = (
        P(("grp", "mem"), None, None, None),
        P(("grp", "mem"), None, None),
        P(("grp", "mem"), None),
        P(("grp", "mem")),
    )
    out_specs = (P(("grp", "mem"), None, None, None), P("grp", "mem", None))
    return jax.shard_map(local, mesh=mesh, in_specs=in_specs, out_specs=out_specs, check_vma=False)
```
